256 devices in a mesh: fibre: 64 (over y_lo, x, z), seg: 4 (over y_hi, core).
Axes of the slice: x: 4, y: 4 (y_hi: 2, y_lo: 2; y = y_hi * 2 + y_lo), z: 8, core: 2. Of those that a mesh axis runs over, the one named last changes fastest.
Arguments:
- strain: float32 [6144, 2048], P(('fibre', 'seg')), may hold values from -500 to 500
- fir_taps: float32 [64], replicated, may hold values from -0.75 to 0.75
- space_taps: float32 [31], replicated, may hold values from -1.2 to 1.2
- sources: int32 [3, 4], replicated, may hold values from 0 to 6143, as said below
Outputs:
- correlations: float32 [3, 4, 6144, 256], P(None, None, ('fibre', 'seg'))
The draws below stay inside these ranges and needn't reach their ends.
Inputs may be any that keep to these rules, and one draw needn't show every extreme that they name: `sources`: virtual-source channel indices; repeats are allowed.
All inputs are finite; a program needn't handle non-finite values.
Results may differ from the reference program's by a relative error of at most 0.0028.
Values may be sent and summed in bfloat16 or wider, within the bound.
A program may use at most 64 MiB of HBM per device.

```python
import math
import jax
import jax.numpy as jnp
from jax import lax

CH_DEV = 24
SAMPLES = 2048
TAPS = 64
HALF = 15
RUN = 64
LAGS = 256
PANELS = 3
SRC = 4
CHANNELS = 6144


def draw_strain(key, part):
    key_base, key_rows, key_blocks = jax.random.split(key, 3)
    base = jnp.clip(jax.random.normal(key_base, (CHANNELS, SAMPLES), jnp.float32), -6.0, 6.0)
    row_scale = jnp.exp(jax.random.uniform(key_rows, (CHANNELS, 1), jnp.float32, 0.0, math.log(10.0)))
    block_scale = jnp.exp(jax.random.uniform(key_blocks, (1, SAMPLES // 64), jnp.float32, 0.0, math.log(4.0)))
    column_scale = jnp.repeat(block_scale, 64, axis=1)
    return (base * row_scale * column_scale).astype(jnp.float32)


def draw_sources(key, part):
    key_centre, key_offset = jax.random.split(jax.random.fold_in(key, 7), 2)
    centres = jax.random.randint(key_centre, (PANELS, 1), 0, CHANNELS)
    offsets = jax.random.randint(key_offset, (PANELS, SRC), 0, 4 * CH_DEV)
    chosen = (centres + offsets) % CHANNELS
    chosen = chosen.at[0, 0].set(0)
    chosen = chosen.at[PANELS - 1, SRC - 1].set(CHANNELS - 1)
    return chosen.astype(jnp.int32)


def gaussian(key, extent, deviation, bound, dtype=jnp.bfloat16):
    values = deviation * jax.random.normal(key, extent, jnp.float32)
    return jnp.clip(values, min=-bound, max=bound).astype(dtype)


def setup_inputs(seed: int = 0) -> dict:
    seeds = jax.random.split(jax.random.key(seed), 5)
    strain = draw_strain(jax.random.fold_in(seeds[4], 71), 0)
    fir_taps = gaussian(seeds[1], (TAPS,), 0.125, 0.75, jnp.float32)
    space_taps = gaussian(seeds[2], (2 * HALF + 1,), 0.2, 1.2, jnp.float32)
    sources = draw_sources(jax.random.fold_in(seeds[4], 71), 0)
    return {"strain": strain, "fir_taps": fir_taps, "space_taps": space_taps, "sources": sources}


def reference(strain, fir_taps, space_taps, sources):
    channel_count = strain.shape[0]
    sample_count = strain.shape[1]
    padded = jnp.pad(strain, ((0, 0), (TAPS - 1, 0)))

    def fir_step(shift_index, accum):
        piece = lax.dynamic_slice_in_dim(padded, TAPS - 1 - shift_index, sample_count, 1)
        return accum + fir_taps[shift_index] * piece

    filtered = lax.fori_loop(0, TAPS, fir_step, jnp.zeros(strain.shape, jnp.float32))
    padded_rows = jnp.pad(filtered, ((HALF, HALF), (0, 0)))

    def space_step(shift_index, accum):
        piece = lax.dynamic_slice_in_dim(padded_rows, shift_index, channel_count, 0)
        return accum + space_taps[shift_index] * piece

    smoothed = lax.fori_loop(0, 2 * HALF + 1, space_step, jnp.zeros(strain.shape, jnp.float32))
    magnitude = jnp.pad(jnp.abs(smoothed), ((0, 0), (RUN, RUN)))

    def run_step(shift_index, accum):
        return accum + lax.dynamic_slice_in_dim(magnitude, shift_index, sample_count, 1)

    window_sum = lax.fori_loop(0, 2 * RUN + 1, run_step, jnp.zeros(strain.shape, jnp.float32))
    positions = jnp.arange(sample_count)
    window_count = (jnp.minimum(positions, RUN) + jnp.minimum(sample_count - 1 - positions, RUN) + 1).astype(jnp.float32)
    level = window_sum / window_count[None, :]
    normed = (smoothed / (level + 1e-5)).astype(jnp.bfloat16)
    length = sample_count + LAGS
    spectra = jnp.fft.rfft(normed.astype(jnp.float32), length, axis=1)
    flat_sources = sources.reshape(-1).astype(jnp.int32)
    norm_factor = float(sample_count) ** -0.5

    def correlate(channel):
        record = jnp.take(normed, channel, axis=0).astype(jnp.float32)
        source_spectrum = jnp.fft.rfft(record, length)
        circular = jnp.fft.irfft(jnp.conj(source_spectrum)[None, :] * spectra, length, axis=1)
        kept = jnp.concatenate([circular[:, length - LAGS // 2:], circular[:, :LAGS // 2]], axis=1)
        return (kept * norm_factor).astype(jnp.float32)

    result = lax.map(correlate, flat_sources)
    return result.reshape(PANELS, SRC, channel_count, LAGS)
```

```python
import functools

import jax
import jax.numpy as jnp
from jax import lax
from jax.experimental import pallas as pl
from jax.experimental.pallas import tpu as pltpu
from jax.sharding import PartitionSpec as P

MESH = pl.DeviceIdType.MESH
F32 = jnp.float32
BF16 = jnp.bfloat16

CH = 24
BLOCKS = 16
SAMPLES = BLOCKS * 128
TAPS = 64
SPACE = 31
HALF = 15
RUN = 64
SRCS = 12
SROWS = 16
FINE = 16
COARSE = 8
PIECES = 32


def source_row(i):
    return i if i < 6 else i + 2


def dot(a, b, contract=((1,), (0,))):
    return lax.dot_general(a, b, (contract, ((), ())), preferred_element_type=F32)


def split(x):
    high = x.astype(BF16)
    return high, (x - high.astype(F32)).astype(BF16)


def iota(shape, dim):
    return lax.broadcasted_iota(jnp.int32, shape, dim)


def three_pass_weights(w, part):
    high, low = split(w)
    picked = jnp.where(part == 1, low.astype(F32), high.astype(F32))
    return picked.astype(BF16)


def source_weights(src_ref, space_ref, first):
    shape = (SROWS, 128)
    row, lane = iota(shape, 0), iota(shape, 1)
    chosen = jnp.full(shape, -(1 << 20), jnp.int32)
    for i in range(SRCS):
        chosen = jnp.where(row == source_row(i), src_ref[i // 4, i % 4], chosen)
    part, r = lane // 32, lane % 32
    tap = jnp.where(r < CH, first + r - chosen + HALF, -1)
    w = jnp.zeros(shape, F32)
    for k in range(SPACE):
        w = jnp.where(tap == k, space_ref[k], w)
    return three_pass_weights(w, part)[:, :96]


def own_weights(space_ref, first, channels):
    shape = (CH, 256)
    row, lane = iota(shape, 0), iota(shape, 1)
    part, r = lane // 64, lane % 64
    rel = jnp.where(r < 32, r, jnp.where(r < 48, r - 48, r - 24))
    inside = (first + rel >= 0) & (first + rel < channels) & ((r < CH) | (r >= 32))
    tap = jnp.where(inside, rel - row + HALF, -1)
    w = jnp.zeros(shape, F32)
    for k in range(SPACE):
        w = jnp.where(tap == k, space_ref[k], w)
    return three_pass_weights(w, part)[:, :192]


def fir_weights(fir_ref):
    lane = iota((8, 128), 1)
    v = jnp.zeros((8, 128), F32)
    for k in range(TAPS):
        v = jnp.where(lane == k, fir_ref[k], v)
    turned = pltpu.roll(
        jnp.broadcast_to(v[0:1], (128, 128)), 0, 1, stride=1, stride_axis=0
    )
    u, t = iota((128, 128), 0), iota((128, 128), 1)
    now = jnp.where(t >= u, turned, 0.0)
    later = jnp.where(t < u, turned, 0.0)
    high, low = split(jnp.concatenate([now, later], axis=1))
    return jnp.concatenate([high, high, low], axis=0)


def window_weights():
    u, t = iota((128, 128), 0), iota((128, 128), 1)
    here = jnp.abs(u - t) <= RUN
    after = u - t >= RUN
    before = t - u >= RUN
    one = jnp.concatenate(
        [jnp.where(m, 1.0, 0.0).astype(F32) for m in (here, after, before)], axis=1
    ).astype(BF16)
    return jnp.concatenate([one, one], axis=0)


def normalized(x, rows, fir_w, win_w):
    high, low = split(x)
    g = dot(jnp.concatenate([high, low, high], axis=1), fir_w)
    zero = jnp.zeros((rows, 128), F32)
    smooth = g[:, :128] + jnp.concatenate([zero, g[:-rows, 128:]], axis=0)
    high, low = split(jnp.abs(smooth))
    g = dot(jnp.concatenate([high, low], axis=1), win_w)
    total = (
        g[:, :128]
        + jnp.concatenate([zero, g[:-rows, 128:256]], axis=0)
        + jnp.concatenate([g[rows:, 256:], zero], axis=0)
    )
    t = iota((rows, 128), 1)
    first = (jnp.minimum(t, RUN) + (RUN + 1)).astype(F32)
    last = (jnp.minimum(127 - t, RUN) + (RUN + 1)).astype(F32)
    level = jnp.concatenate(
        [
            total[:rows] / first,
            total[rows:-rows] * (1.0 / (2 * RUN + 1)),
            total[-rows:] / last,
        ],
        axis=0,
    )
    return smooth / (level + 1e-5)


def kernel(
    nf, ns, nz,
    fir_ref, space_ref, src_ref, strain_ref, out_ref,
    x_ref, halo_ref, send1, recv1, send2, recv2, gathered,
    fir_w, win_w, own_w, n_ref, s_ref, q_ref, a_ref,
    load_sem, sems, halo_sems,
):
    nq = (nf // nz) * ns
    own = PIECES // nq
    f, g = lax.axis_index("fibre"), lax.axis_index("seg")
    plane = lax.div(f, nz) * ns + g
    z = lax.rem(f, nz)
    line = f * ns + g
    count = nf * ns

    def in_plane(step):
        other = lax.rem(plane + step, nq)
        return (lax.div(other, ns) * nz + z, lax.rem(other, ns)), other

    def along_z(step):
        return (lax.div(f, nz) * nz + lax.rem(z + step, nz), g)

    def on_line(step):
        other = lax.rem(line + step + count, count)
        return (lax.div(other, ns), lax.rem(other, ns))

    load = pltpu.make_async_copy(strain_ref, x_ref, load_sem)
    load.start()
    gathered[...] = jnp.zeros_like(gathered)
    barrier = pltpu.get_barrier_semaphore()

    @pl.loop(1, nq)
    def _(step):
        pl.semaphore_signal(barrier, inc=1, device_id=in_plane(step)[0], device_id_type=MESH)

    @pl.loop(1, nz)
    def _(step):
        pl.semaphore_signal(barrier, inc=1, device_id=along_z(step), device_id_type=MESH)

    for step in (-1, 1):
        pl.semaphore_signal(barrier, inc=1, device_id=on_line(step), device_id_type=MESH)

    first_channel = line * CH
    source_w = source_weights(src_ref, space_ref, first_channel)
    load.wait()
    pad = jnp.zeros((8, SAMPLES), F32)
    high, low = split(jnp.concatenate([x_ref[...], pad], axis=0))
    part = dot(source_w, jnp.concatenate([high, high, low], axis=0))
    for b in range(BLOCKS):
        for h in range(2):
            send1[2 * b + h] = part[8 * h : 8 * h + 8, 128 * b : 128 * b + 128]

    pl.semaphore_wait(barrier, nq - 1 + nz - 1 + 2)

    def plane_copy(step):
        device, other = in_plane(step)
        return pltpu.make_async_remote_copy(
            src_ref=send1.at[pl.ds(other * own, own), pl.ds(0, 6)],
            dst_ref=recv1.at[step, :, pl.ds(0, 6)],
            send_sem=sems.at[0], recv_sem=sems.at[1],
            device_id=device, device_id_type=MESH,
        )

    def z_copy(step):
        return pltpu.make_async_remote_copy(
            src_ref=send2.at[:, pl.ds(0, 6)],
            dst_ref=recv2.at[step, :, pl.ds(0, 6)],
            send_sem=sems.at[2], recv_sem=sems.at[3],
            device_id=along_z(step), device_id_type=MESH,
        )

    def gather_copy(step):
        mine = gathered.at[pl.ds(plane * own, own), pl.ds(0, 6)]
        return pltpu.make_async_remote_copy(
            src_ref=mine, dst_ref=mine,
            send_sem=sems.at[4], recv_sem=sems.at[5],
            device_id=in_plane(step)[0], device_id_type=MESH,
        )

    def bulk(ref, first, device):
        return pltpu.make_async_remote_copy(
            src_ref=ref, dst_ref=ref,
            send_sem=sems.at[first], recv_sem=sems.at[first + 1],
            device_id=device, device_id_type=MESH,
        )

    up = pltpu.make_async_remote_copy(
        src_ref=x_ref.at[pl.ds(CH - 16, 16)], dst_ref=halo_ref.at[0],
        send_sem=halo_sems.at[0], recv_sem=halo_sems.at[1],
        device_id=on_line(1), device_id_type=MESH,
    )
    down = pltpu.make_async_remote_copy(
        src_ref=x_ref.at[pl.ds(0, 16)], dst_ref=halo_ref.at[1],
        send_sem=halo_sems.at[2], recv_sem=halo_sems.at[3],
        device_id=on_line(-1), device_id_type=MESH,
    )

    @pl.loop(1, nq)
    def _(step):
        plane_copy(step).start()

    fir_w[...] = fir_weights(fir_ref)
    win_w[...] = window_weights()
    own_w[...] = own_weights(space_ref, first_channel, count * CH)
    a_ref[SRCS * FINE :, :] = jnp.zeros((256 - SRCS * FINE, a_ref.shape[1]), BF16)

    all_plane = bulk(recv1.at[pl.ds(1, nq - 1), :, pl.ds(0, 6)], 0, in_plane(1)[0])
    all_z = bulk(recv2.at[pl.ds(1, nz - 1), :, pl.ds(0, 6)], 2, along_z(1))
    all_gather = bulk(gathered.at[pl.ds(0, (nq - 1) * own), pl.ds(0, 6)], 4, in_plane(1)[0])

    all_plane.wait_recv()
    total = send1[pl.ds(plane * own, own), 0:6, :]
    for step in range(1, nq):
        total = total + recv1[step, :, 0:6, :]
    send2[:, 0:6, :] = total

    @pl.loop(1, nz)
    def _(step):
        z_copy(step).start()

    up.start()
    down.start()

    all_z.wait_recv()
    for step in range(1, nz):
        total = total + recv2[step, :, 0:6, :]
    gathered[pl.ds(plane * own, own), 0:6, :] = total

    @pl.loop(1, nq)
    def _(step):
        gather_copy(step).start()

    up.wait_recv()
    down.wait_recv()
    high, low = split(jnp.concatenate([x_ref[...], pad, halo_ref[0], halo_ref[1]], axis=0))
    spatial = dot(own_w[...], jnp.concatenate([high, high, low], axis=0))
    blocks = jnp.concatenate(
        [spatial[:, 128 * b : 128 * b + 128] for b in range(BLOCKS)], axis=0
    )
    n_ref[...] = normalized(blocks, CH, fir_w[...], win_w[...])
    lane = iota((CH, 128), 1)
    none = [jnp.zeros((CH, 128), F32)] * COARSE

    def turned_blocks(b):
        if not 0 <= b < BLOCKS:
            return none
        block = n_ref[b * CH : b * CH + CH]
        return [block] + [pltpu.roll(block, 128 - 16 * k, 1) for k in range(1, COARSE)]

    here = none
    for b in range(-1, BLOCKS + 1):
        following = turned_blocks(b + 1)
        shifted = [
            jnp.where(lane < 128 - 16 * k, here[k], following[k]) for k in range(COARSE)
        ]
        q_ref[:, (b + 1) * 128 : (b + 2) * 128] = jnp.concatenate(shifted, axis=0).astype(BF16)
        here = following

    all_gather.wait_recv()
    records = gathered[...].reshape(BLOCKS * SROWS, 128)
    s_ref[...] = normalized(records, SROWS, fir_w[...], win_w[...])
    shift, lane = iota((FINE, 128), 0), iota((FINE, 128), 1)
    for i in range(SRCS):
        before = jnp.zeros((FINE, 128), F32)
        for b in range(BLOCKS + 1):
            if b < BLOCKS:
                row = b * SROWS + source_row(i)
                wide = jnp.broadcast_to(s_ref[row : row + 1, :], (FINE, 128))
                here = pltpu.roll(wide, 0, 1, stride=1, stride_axis=0)
            else:
                here = jnp.zeros((FINE, 128), F32)
            a_ref[FINE * i : FINE * i + FINE, 128 * b : 128 * b + 128] = jnp.where(
                lane >= shift, here, before
            ).astype(BF16)
            before = here

    width = (BLOCKS + 1) * 128
    lane = iota((CH, 128), 1)
    factor = float(SAMPLES) ** -0.5
    for half in range(2):
        d = dot(q_ref[:, 128 * half : 128 * half + width], a_ref[...], ((1,), (1,)))
        for tile in range(2):
            v = [
                d[CH * k : CH * k + CH, 128 * tile : 128 * tile + 128] * factor
                for k in range(COARSE)
            ]
            for bit in (1, 2, 4):
                low_part = (lax.div(lane, 16) & bit) == 0
                for k in range(COARSE):
                    if k & bit:
                        continue
                    a, b = v[k], v[k | bit]
                    v[k] = jnp.where(low_part, a, pltpu.roll(b, 16 * bit, 1))
                    v[k | bit] = jnp.where(low_part, pltpu.roll(a, 128 - 16 * bit, 1), b)
            for k in range(COARSE):
                if COARSE * tile + k < SRCS:
                    out_ref[COARSE * tile + k, :, 128 * half : 128 * half + 128] = v[k]

    all_plane.wait_send()
    all_z.wait_send()
    all_gather.wait_send()
    up.wait_send()
    down.wait_send()


def local(nf, ns, nz, strain, fir_taps, space_taps, sources):
    nq = (nf // nz) * ns
    own = PIECES // nq
    width = (BLOCKS + 1) * 128
    smem = pl.BlockSpec(memory_space=pltpu.SMEM)
    out = pl.pallas_call(
        functools.partial(kernel, nf, ns, nz),
        out_shape=jax.ShapeDtypeStruct((SRCS, CH, 2 * 128), F32),
        in_specs=[smem, smem, smem, pl.BlockSpec(memory_space=pl.ANY)],
        out_specs=pl.BlockSpec(memory_space=pltpu.VMEM),
        scratch_shapes=[
            pltpu.VMEM((CH, SAMPLES), F32),
            pltpu.VMEM((2, 16, SAMPLES), F32),
            pltpu.VMEM((PIECES, 8, 128), F32),
            pltpu.VMEM((nq, own, 8, 128), F32),
            pltpu.VMEM((own, 8, 128), F32),
            pltpu.VMEM((nz, own, 8, 128), F32),
            pltpu.VMEM((PIECES, 8, 128), F32),
            pltpu.VMEM((384, 256), BF16),
            pltpu.VMEM((256, 384), BF16),
            pltpu.VMEM((CH, 192), BF16),
            pltpu.VMEM((BLOCKS * CH, 128), F32),
            pltpu.VMEM((BLOCKS * SROWS, 128), F32),
            pltpu.VMEM((COARSE * CH, width + 128), BF16),
            pltpu.VMEM((256, width), BF16),
            pltpu.SemaphoreType.DMA,
            pltpu.SemaphoreType.DMA((6,)),
            pltpu.SemaphoreType.DMA((4,)),
        ],
        compiler_params=pltpu.CompilerParams(collective_id=0, has_side_effects=True),
    )(fir_taps, space_taps, sources, strain)
    return out.reshape(3, 4, CH, 256)


def solution(mesh):
    nf, ns = mesh.shape["fibre"], mesh.shape["seg"]
    nz = 8 if nf % 8 == 0 else 2
    return jax.shard_map(
        functools.partial(local, nf, ns, nz),
        mesh=mesh,
        in_specs=(P(("fibre", "seg"), None), P(), P(), P()),
        out_specs=P(None, None, ("fibre", "seg"), None),
        check_vma=False,
    )
```

```python
import functools

import jax
import jax.numpy as jnp
from jax import lax
from jax.experimental import pallas as pl
from jax.experimental.pallas import tpu as pltpu
from jax.sharding import PartitionSpec as P

MESH = pl.DeviceIdType.MESH
F32 = jnp.float32
BF16 = jnp.bfloat16

CH = 24
BLOCKS = 16
SAMPLES = BLOCKS * 128
TAPS = 64
SPACE = 31
HALF = 15
RUN = 64
SRCS = 12
SROWS = 16
FINE = 16
COARSE = 8
PIECES = 32


def source_row(i):
    return i if i < 6 else i + 2


def dot(a, b, contract=((1,), (0,))):
    return lax.dot_general(a, b, (contract, ((), ())), preferred_element_type=F32)


def split(x):
    high = x.astype(BF16)
    return high, (x - high.astype(F32)).astype(BF16)


def iota(shape, dim):
    return lax.broadcasted_iota(jnp.int32, shape, dim)


def three_pass_weights(w, part):
    high, low = split(w)
    picked = jnp.where(part == 1, low.astype(F32), high.astype(F32))
    return picked.astype(BF16)


def source_weights(src_ref, space_ref, first):
    shape = (SROWS, 128)
    row, lane = iota(shape, 0), iota(shape, 1)
    chosen = jnp.full(shape, -(1 << 20), jnp.int32)
    for i in range(SRCS):
        chosen = jnp.where(row == source_row(i), src_ref[i // 4, i % 4], chosen)
    part, r = lane // 32, lane % 32
    tap = jnp.where(r < CH, first + r - chosen + HALF, -1)
    w = jnp.zeros(shape, F32)
    for k in range(SPACE):
        w = jnp.where(tap == k, space_ref[k], w)
    return three_pass_weights(w, part)[:, :96]


def own_weights(space_ref, first, channels):
    shape = (CH, 256)
    row, lane = iota(shape, 0), iota(shape, 1)
    part, r = lane // 64, lane % 64
    rel = jnp.where(r < 32, r, jnp.where(r < 48, r - 48, r - 24))
    inside = (first + rel >= 0) & (first + rel < channels) & ((r < CH) | (r >= 32))
    tap = jnp.where(inside, rel - row + HALF, -1)
    w = jnp.zeros(shape, F32)
    for k in range(SPACE):
        w = jnp.where(tap == k, space_ref[k], w)
    return three_pass_weights(w, part)[:, :192]


def fir_weights(fir_ref):
    lane = iota((8, 128), 1)
    v = jnp.zeros((8, 128), F32)
    for k in range(TAPS):
        v = jnp.where(lane == k, fir_ref[k], v)
    turned = pltpu.roll(
        jnp.broadcast_to(v[0:1], (128, 128)), 0, 1, stride=1, stride_axis=0
    )
    u, t = iota((128, 128), 0), iota((128, 128), 1)
    now = jnp.where(t >= u, turned, 0.0)
    later = jnp.where(t < u, turned, 0.0)
    high, low = split(jnp.concatenate([now, later], axis=1))
    return jnp.concatenate([high, high, low], axis=0)


def window_weights():
    u, t = iota((128, 128), 0), iota((128, 128), 1)
    here = jnp.abs(u - t) <= RUN
    after = u - t >= RUN
    before = t - u >= RUN
    one = jnp.concatenate(
        [jnp.where(m, 1.0, 0.0).astype(F32) for m in (here, after, before)], axis=1
    ).astype(BF16)
    return jnp.concatenate([one, one], axis=0)


def normalized(x, rows, fir_w, win_w):
    high, low = split(x)
    g = dot(jnp.concatenate([high, low, high], axis=1), fir_w)
    zero = jnp.zeros((rows, 128), F32)
    smooth = g[:, :128] + jnp.concatenate([zero, g[:-rows, 128:]], axis=0)
    high, low = split(jnp.abs(smooth))
    g = dot(jnp.concatenate([high, low], axis=1), win_w)
    total = (
        g[:, :128]
        + jnp.concatenate([zero, g[:-rows, 128:256]], axis=0)
        + jnp.concatenate([g[rows:, 256:], zero], axis=0)
    )
    t = iota((rows, 128), 1)
    first = (jnp.minimum(t, RUN) + (RUN + 1)).astype(F32)
    last = (jnp.minimum(127 - t, RUN) + (RUN + 1)).astype(F32)
    level = jnp.concatenate(
        [
            total[:rows] / first,
            total[rows:-rows] * (1.0 / (2 * RUN + 1)),
            total[-rows:] / last,
        ],
        axis=0,
    )
    return smooth / (level + 1e-5)


def ring(step, size):
    return min(step % size, -step % size)


def plane_steps(nx):
    steps = [(dy, dx, dc) for dy in range(4) for dx in range(nx) for dc in range(2)][1:]
    return sorted(steps, key=lambda s: (-ring(s[0], 4) - ring(s[1], nx), s[2]))


def z_steps(nz):
    return sorted(range(1, nz), key=lambda s: -ring(s, nz))


def kernel(
    nf, ns, nz,
    fir_hbm, space_hbm, src_hbm, strain_ref, out_ref,
    fir_ref, space_ref, src_ref,
    x_ref, halo_ref, send1, recv1, send2, recv2, gathered,
    fir_w, win_w, own_w, n_ref, s_ref, q_ref, a_ref,
    load_sem, sems, halo_sems,
):
    nq = (nf // nz) * ns
    nx = nf // nz // 2
    own = PIECES // nq
    f, g = lax.axis_index("fibre"), lax.axis_index("seg")
    z, row = lax.rem(f, nz), lax.div(f, nz)
    x, core = lax.rem(row, nx), lax.rem(g, 2)
    y = lax.div(g, 2) * 2 + lax.div(row, nx)
    line = f * ns + g
    count = nf * ns

    ys = [lax.rem(y + step, 4) for step in range(4)]
    xs = [lax.rem(x + step, nx) for step in range(nx)]
    cores = [core, 1 - core]
    y_fibre = [lax.rem(v, 2) * (nx * nz) + z for v in ys]
    y_seg = [lax.div(v, 2) * 2 for v in ys]
    plane_list = plane_steps(nx)
    z_list = z_steps(nz)

    def in_plane(step):
        dy, dx, dc = step
        return (y_fibre[dy] + xs[dx] * nz, y_seg[dy] + cores[dc])

    def place(step):
        dy, dx, dc = step
        return (ys[dy] * nx + xs[dx]) * 2 + cores[dc]

    plane = place((0, 0, 0))

    def along_z(step):
        return (f - z + lax.rem(z + step, nz), g)

    def on_line(step):
        other = lax.rem(line + step + count, count)
        return (lax.div(other, ns), lax.rem(other, ns))

    loads = [
        pltpu.make_async_copy(src, dst, load_sem.at[i])
        for i, (src, dst) in enumerate(
            [(strain_ref, x_ref), (space_hbm, space_ref), (src_hbm, src_ref), (fir_hbm, fir_ref)]
        )
    ]
    for load in loads:
        load.start()
    barrier = pltpu.get_barrier_semaphore()
    partners = [in_plane(s) for s in plane_list] + [along_z(s) for s in z_list]
    for device in partners + [on_line(-1), on_line(1)]:
        pl.semaphore_signal(barrier, inc=1, device_id=device, device_id_type=MESH)
    gathered[...] = jnp.zeros_like(gathered)

    first_channel = line * CH
    loads[1].wait()
    loads[2].wait()
    source_w = source_weights(src_ref, space_ref, first_channel)
    loads[0].wait()
    pad = jnp.zeros((8, SAMPLES), F32)
    high, low = split(jnp.concatenate([x_ref[...], pad], axis=0))
    part = dot(source_w, jnp.concatenate([high, high, low], axis=0))
    for b in range(BLOCKS):
        for h in range(2):
            send1[2 * b + h] = part[8 * h : 8 * h + 8, 128 * b : 128 * b + 128]

    pl.semaphore_wait(barrier, nq - 1 + nz - 1 + 2)

    def plane_copy(slot, step):
        return pltpu.make_async_remote_copy(
            src_ref=send1.at[pl.ds(place(step) * own, own), pl.ds(0, 6)],
            dst_ref=recv1.at[slot, :, pl.ds(0, 6)],
            send_sem=sems.at[0], recv_sem=sems.at[1],
            device_id=in_plane(step), device_id_type=MESH,
        )

    def z_copy(slot, step):
        return pltpu.make_async_remote_copy(
            src_ref=send2.at[:, pl.ds(0, 6)],
            dst_ref=recv2.at[slot, :, pl.ds(0, 6)],
            send_sem=sems.at[2], recv_sem=sems.at[3],
            device_id=along_z(step), device_id_type=MESH,
        )

    def gather_copy(step):
        mine = gathered.at[pl.ds(plane * own, own), pl.ds(0, 6)]
        return pltpu.make_async_remote_copy(
            src_ref=mine, dst_ref=mine,
            send_sem=sems.at[4], recv_sem=sems.at[5],
            device_id=in_plane(step), device_id_type=MESH,
        )

    def bulk(ref, first, device):
        return pltpu.make_async_remote_copy(
            src_ref=ref, dst_ref=ref,
            send_sem=sems.at[first], recv_sem=sems.at[first + 1],
            device_id=device, device_id_type=MESH,
        )

    up = pltpu.make_async_remote_copy(
        src_ref=x_ref.at[pl.ds(CH - 16, 16)], dst_ref=halo_ref.at[0],
        send_sem=halo_sems.at[0], recv_sem=halo_sems.at[1],
        device_id=on_line(1), device_id_type=MESH,
    )
    down = pltpu.make_async_remote_copy(
        src_ref=x_ref.at[pl.ds(0, 16)], dst_ref=halo_ref.at[1],
        send_sem=halo_sems.at[2], recv_sem=halo_sems.at[3],
        device_id=on_line(-1), device_id_type=MESH,
    )

    for slot, step in enumerate(plane_list):
        plane_copy(slot, step).start()

    loads[3].wait()
    fir_w[...] = fir_weights(fir_ref)
    win_w[...] = window_weights()
    own_w[...] = own_weights(space_ref, first_channel, count * CH)
    a_ref[SRCS * FINE :, :] = jnp.zeros((256 - SRCS * FINE, a_ref.shape[1]), BF16)

    peer = in_plane(plane_list[0])
    all_plane = bulk(recv1.at[:, :, pl.ds(0, 6)], 0, peer)
    all_z = bulk(recv2.at[:, :, pl.ds(0, 6)], 2, along_z(1))
    all_gather = bulk(gathered.at[pl.ds(0, (nq - 1) * own), pl.ds(0, 6)], 4, peer)

    all_plane.wait_recv()
    total = send1[pl.ds(plane * own, own), 0:6, :]
    for slot in range(nq - 1):
        total = total + recv1[slot, :, 0:6, :]
    send2[:, 0:6, :] = total

    for slot, step in enumerate(z_list):
        z_copy(slot, step).start()

    up.start()
    down.start()

    all_z.wait_recv()
    for slot in range(nz - 1):
        total = total + recv2[slot, :, 0:6, :]
    gathered[pl.ds(plane * own, own), 0:6, :] = total

    for step in plane_list:
        gather_copy(step).start()

    up.wait_recv()
    down.wait_recv()
    high, low = split(jnp.concatenate([x_ref[...], pad, halo_ref[0], halo_ref[1]], axis=0))
    spatial = dot(own_w[...], jnp.concatenate([high, high, low], axis=0))
    blocks = jnp.concatenate(
        [spatial[:, 128 * b : 128 * b + 128] for b in range(BLOCKS)], axis=0
    )
    n_ref[...] = normalized(blocks, CH, fir_w[...], win_w[...])
    lane = iota((CH, 128), 1)
    none = [jnp.zeros((CH, 128), F32)] * COARSE

    def turned_blocks(b):
        if not 0 <= b < BLOCKS:
            return none
        block = n_ref[b * CH : b * CH + CH]
        return [block] + [pltpu.roll(block, 128 - 16 * k, 1) for k in range(1, COARSE)]

    here = none
    for b in range(-1, BLOCKS + 1):
        following = turned_blocks(b + 1)
        shifted = [
            jnp.where(lane < 128 - 16 * k, here[k], following[k]) for k in range(COARSE)
        ]
        q_ref[:, (b + 1) * 128 : (b + 2) * 128] = jnp.concatenate(shifted, axis=0).astype(BF16)
        here = following

    all_gather.wait_recv()
    records = gathered[...].reshape(BLOCKS * SROWS, 128)
    s_ref[...] = normalized(records, SROWS, fir_w[...], win_w[...])
    shift, lane = iota((FINE, 128), 0), iota((FINE, 128), 1)
    for i in range(SRCS):
        before = jnp.zeros((FINE, 128), F32)
        for b in range(BLOCKS + 1):
            if b < BLOCKS:
                row = b * SROWS + source_row(i)
                wide = jnp.broadcast_to(s_ref[row : row + 1, :], (FINE, 128))
                here = pltpu.roll(wide, 0, 1, stride=1, stride_axis=0)
            else:
                here = jnp.zeros((FINE, 128), F32)
            a_ref[FINE * i : FINE * i + FINE, 128 * b : 128 * b + 128] = jnp.where(
                lane >= shift, here, before
            ).astype(BF16)
            before = here

    width = (BLOCKS + 1) * 128
    lane = iota((CH, 128), 1)
    factor = float(SAMPLES) ** -0.5
    for half in range(2):
        d = dot(q_ref[:, 128 * half : 128 * half + width], a_ref[...], ((1,), (1,)))
        for tile in range(2):
            v = [
                d[CH * k : CH * k + CH, 128 * tile : 128 * tile + 128] * factor
                for k in range(COARSE)
            ]
            for bit in (1, 2, 4):
                low_part = (lax.div(lane, 16) & bit) == 0
                for k in range(COARSE):
                    if k & bit:
                        continue
                    a, b = v[k], v[k | bit]
                    v[k] = jnp.where(low_part, a, pltpu.roll(b, 16 * bit, 1))
                    v[k | bit] = jnp.where(low_part, pltpu.roll(a, 128 - 16 * bit, 1), b)
            for k in range(COARSE):
                if COARSE * tile + k < SRCS:
                    out_ref[COARSE * tile + k, :, 128 * half : 128 * half + 128] = v[k]

    all_plane.wait_send()
    all_z.wait_send()
    all_gather.wait_send()
    up.wait_send()
    down.wait_send()


def copy_out(in_ref, out_ref, sem):
    copy = pltpu.make_async_copy(in_ref, out_ref, sem)
    copy.start()
    copy.wait()


def local(nf, ns, nz, strain, fir_taps, space_taps, sources):
    nq = (nf // nz) * ns
    own = PIECES // nq
    width = (BLOCKS + 1) * 128
    hbm = pl.BlockSpec(memory_space=pltpu.HBM)
    result = jax.ShapeDtypeStruct((SRCS, CH, 2 * 128), F32)
    out = pl.pallas_call(
        functools.partial(kernel, nf, ns, nz),
        out_shape=result,
        in_specs=[hbm] * 4,
        out_specs=pl.BlockSpec(memory_space=pltpu.VMEM),
        scratch_shapes=[
            pltpu.SMEM((TAPS,), F32),
            pltpu.SMEM((SPACE,), F32),
            pltpu.SMEM((3, 4), jnp.int32),
            pltpu.VMEM((CH, SAMPLES), F32),
            pltpu.VMEM((2, 16, SAMPLES), F32),
            pltpu.VMEM((PIECES, 8, 128), F32),
            pltpu.VMEM((nq - 1, own, 8, 128), F32),
            pltpu.VMEM((own, 8, 128), F32),
            pltpu.VMEM((nz - 1, own, 8, 128), F32),
            pltpu.VMEM((PIECES, 8, 128), F32),
            pltpu.VMEM((384, 256), BF16),
            pltpu.VMEM((256, 384), BF16),
            pltpu.VMEM((CH, 192), BF16),
            pltpu.VMEM((BLOCKS * CH, 128), F32),
            pltpu.VMEM((BLOCKS * SROWS, 128), F32),
            pltpu.VMEM((COARSE * CH, width + 128), BF16),
            pltpu.VMEM((256, width), BF16),
            pltpu.SemaphoreType.DMA((4,)),
            pltpu.SemaphoreType.DMA((6,)),
            pltpu.SemaphoreType.DMA((4,)),
        ],
        compiler_params=pltpu.CompilerParams(
            collective_id=0, has_side_effects=True, vmem_limit_bytes=16 << 20
        ),
    )(*[pltpu.with_memory_space_constraint(v, pltpu.HBM) for v in (fir_taps, space_taps, sources, strain)])
    out = pl.pallas_call(
        copy_out,
        out_shape=result,
        in_specs=[pl.BlockSpec(memory_space=pltpu.VMEM)],
        out_specs=pl.BlockSpec(memory_space=pltpu.HBM),
        scratch_shapes=[pltpu.SemaphoreType.DMA],
        compiler_params=pltpu.CompilerParams(vmem_limit_bytes=16 << 20),
    )(out)
    return out.reshape(3, 4, CH, 256)


def solution(mesh):
    nf, ns = mesh.shape["fibre"], mesh.shape["seg"]
    nz = 8 if nf % 8 == 0 else 2
    return jax.shard_map(
        functools.partial(local, nf, ns, nz),
        mesh=mesh,
        in_specs=(P(("fibre", "seg"), None), P(), P(), P()),
        out_specs=P(None, None, ("fibre", "seg"), None),
        check_vma=False,
    )
```

```python
import functools

import jax
import jax.numpy as jnp
from jax import lax
from jax.experimental import pallas as pl
from jax.experimental.pallas import tpu as pltpu
from jax.sharding import PartitionSpec as P

MESH = pl.DeviceIdType.MESH
F32 = jnp.float32
BF16 = jnp.bfloat16

CH = 24
BLOCKS = 16
SAMPLES = BLOCKS * 128
TAPS = 64
SPACE = 31
HALF = 15
RUN = 64
SRCS = 12
SROWS = 16
FINE = 16
COARSE = 8
PIECES = 24


def dot(a, b, contract=((1,), (0,))):
    return lax.dot_general(a, b, (contract, ((), ())), preferred_element_type=F32)


def split(x):
    high = x.astype(BF16)
    return high, (x - high.astype(F32)).astype(BF16)


def iota(shape, dim):
    return lax.broadcasted_iota(jnp.int32, shape, dim)


def three_pass_weights(w, part):
    high, low = split(w)
    picked = jnp.where(part == 1, low.astype(F32), high.astype(F32))
    return picked.astype(BF16)


def source_weights(src_ref, space_ref, first):
    shape = (SROWS, 128)
    row, lane = iota(shape, 0), iota(shape, 1)
    chosen = jnp.full(shape, -(1 << 20), jnp.int32)
    for i in range(SRCS):
        here = (row == i) if i < 8 else (row == i) | (row == i + 4)
        chosen = jnp.where(here, src_ref[i // 4, i % 4], chosen)
    part, r = lane // 32, lane % 32
    tap = jnp.where(r < CH, first + r - chosen + HALF, -1)
    w = jnp.zeros(shape, F32)
    for k in range(SPACE):
        w = jnp.where(tap == k, space_ref[k], w)
    return three_pass_weights(w, part)[:, :96]


def own_weights(space_ref, first, channels):
    shape = (CH, 256)
    row, lane = iota(shape, 0), iota(shape, 1)
    part, r = lane // 64, lane % 64
    rel = jnp.where(r < 32, r, jnp.where(r < 48, r - 48, r - 24))
    inside = (first + rel >= 0) & (first + rel < channels) & ((r < CH) | (r >= 32))
    tap = jnp.where(inside, rel - row + HALF, -1)
    w = jnp.zeros(shape, F32)
    for k in range(SPACE):
        w = jnp.where(tap == k, space_ref[k], w)
    return three_pass_weights(w, part)[:, :192]


def fir_weights(fir_ref):
    lane = iota((8, 128), 1)
    v = jnp.zeros((8, 128), F32)
    for k in range(TAPS):
        v = jnp.where(lane == k, fir_ref[k], v)
    turned = pltpu.roll(
        jnp.broadcast_to(v[0:1], (128, 128)), 0, 1, stride=1, stride_axis=0
    )
    u, t = iota((128, 128), 0), iota((128, 128), 1)
    now = jnp.where(t >= u, turned, 0.0)
    later = jnp.where(t < u, turned, 0.0)
    high, low = split(jnp.concatenate([now, later], axis=1))
    return jnp.concatenate([high, high, low], axis=0)


def window_weights():
    u, t = iota((128, 128), 0), iota((128, 128), 1)
    here = jnp.abs(u - t) <= RUN
    after = u - t >= RUN
    before = t - u >= RUN
    one = jnp.concatenate(
        [jnp.where(m, 1.0, 0.0).astype(F32) for m in (here, after, before)], axis=1
    ).astype(BF16)
    return jnp.concatenate([one, one], axis=0)


def normalized(x, rows, fir_w, win_w):
    high, low = split(x)
    g = dot(jnp.concatenate([high, low, high], axis=1), fir_w)
    zero = jnp.zeros((rows, 128), F32)
    smooth = g[:, :128] + jnp.concatenate([zero, g[:-rows, 128:]], axis=0)
    high, low = split(jnp.abs(smooth))
    g = dot(jnp.concatenate([high, low], axis=1), win_w)
    total = (
        g[:, :128]
        + jnp.concatenate([zero, g[:-rows, 128:256]], axis=0)
        + jnp.concatenate([g[rows:, 256:], zero], axis=0)
    )
    t = iota((rows, 128), 1)
    first = (jnp.minimum(t, RUN) + (RUN + 1)).astype(F32)
    last = (jnp.minimum(127 - t, RUN) + (RUN + 1)).astype(F32)
    level = jnp.concatenate(
        [
            total[:rows] / first,
            total[rows:-rows] * (1.0 / (2 * RUN + 1)),
            total[-rows:] / last,
        ],
        axis=0,
    )
    return smooth / (level + 1e-5)


def ring(step, size):
    return min(step % size, -step % size)


def plane_steps(nx):
    steps = [(dy, dx, dc) for dy in range(4) for dx in range(nx) for dc in range(2)][1:]
    return sorted(steps, key=lambda s: (-ring(s[0], 4) - ring(s[1], nx), s[2]))


def owner(y, x, nx):
    return lax.div(y, 2) * lax.div(x, 2) if nx > 1 else lax.div(y, 3)


def owner_chip(y, x, nx):
    if nx == 1:
        return y
    half = lax.div(y, 2)
    return (1 - half) * (nx * y + x) + half * (2 * nx + 2 * (y - 2) + x)


def z_steps(nz):
    return sorted(range(1, nz), key=lambda s: -ring(s, nz))


def kernel(
    nf, ns, nz,
    fir_hbm, space_hbm, src_hbm, strain_ref, out_ref,
    fir_ref, space_ref, src_ref,
    x_ref, halo_ref, send1, recv1, send2, recv2, gathered,
    fir_w, win_w, own_w, n_ref, s_ref, q_ref, a_ref,
    load_sem, sems, halo_sems,
):
    nq = (nf // nz) * ns
    nx = nf // nz // 2
    owners = nq * 3 // 4
    own = PIECES // owners
    f, g = lax.axis_index("fibre"), lax.axis_index("seg")
    z, row = lax.rem(f, nz), lax.div(f, nz)
    x, core = lax.rem(row, nx), lax.rem(g, 2)
    y = lax.div(g, 2) * 2 + lax.div(row, nx)
    line = f * ns + g
    count = nf * ns

    ys = [lax.rem(y + step, 4) for step in range(4)]
    xs = [lax.rem(x + step, nx) for step in range(nx)]
    cores = [core, 1 - core]
    y_fibre = [lax.rem(v, 2) * (nx * nz) + z for v in ys]
    y_seg = [lax.div(v, 2) * 2 for v in ys]
    plane_list = plane_steps(nx)
    z_list = z_steps(nz)

    def in_plane(step):
        dy, dx, dc = step
        return (y_fibre[dy] + xs[dx] * nz, y_seg[dy] + cores[dc])

    is_owner = owner(y, x, nx) == 0

    def piece(step):
        dy, dx, dc = step
        return owner_chip(ys[dy], xs[dx], nx) * 2 + cores[dc]

    mine = piece((0, 0, 0))

    def along_z(step):
        return (f - z + lax.rem(z + step, nz), g)

    def on_line(step):
        other = lax.rem(line + step + count, count)
        return (lax.div(other, ns), lax.rem(other, ns))

    loads = [
        pltpu.make_async_copy(src, dst, load_sem.at[i])
        for i, (src, dst) in enumerate(
            [(strain_ref, x_ref), (space_hbm, space_ref), (src_hbm, src_ref), (fir_hbm, fir_ref)]
        )
    ]
    for load in loads:
        load.start()
    barrier = pltpu.get_barrier_semaphore()

    def greet(devices):
        for device in devices:
            pl.semaphore_signal(barrier, inc=1, device_id=device, device_id_type=MESH)

    @pl.when(is_owner)
    def _():
        greet([in_plane(s) for s in plane_list] + [along_z(s) for s in z_list])

    greet([on_line(-1), on_line(1)])

    first_channel = line * CH
    loads[1].wait()
    loads[2].wait()
    source_w = source_weights(src_ref, space_ref, first_channel)
    loads[0].wait()
    pad = jnp.zeros((8, SAMPLES), F32)
    high, low = split(jnp.concatenate([x_ref[...], pad], axis=0))
    part = dot(source_w, jnp.concatenate([high, high, low], axis=0))
    upper = iota((8, 128), 0) < 4
    for b in range(BLOCKS):
        send1[b] = part[:8, 128 * b : 128 * b + 128]
    for b in range(0, BLOCKS, 2):
        send1[BLOCKS + b // 2] = jnp.where(
            upper, part[8:, 128 * b : 128 * b + 128], part[8:, 128 * b + 128 : 128 * b + 256]
        )

    pl.when(is_owner)(lambda: pl.semaphore_wait(barrier, owners - 1 + nz - 1 + 2))
    pl.when(~is_owner)(lambda: pl.semaphore_wait(barrier, owners + 2))

    def plane_copy(slot, step):
        return pltpu.make_async_remote_copy(
            src_ref=send1.at[pl.ds(piece(step) * own, own)],
            dst_ref=recv1.at[slot],
            send_sem=sems.at[0], recv_sem=sems.at[1],
            device_id=in_plane(step), device_id_type=MESH,
        )

    def z_copy(slot, step):
        return pltpu.make_async_remote_copy(
            src_ref=send2,
            dst_ref=recv2.at[slot],
            send_sem=sems.at[2], recv_sem=sems.at[3],
            device_id=along_z(step), device_id_type=MESH,
        )

    def gather_copy(step):
        pieces = gathered.at[pl.ds(mine * own, own)]
        return pltpu.make_async_remote_copy(
            src_ref=pieces, dst_ref=pieces,
            send_sem=sems.at[4], recv_sem=sems.at[5],
            device_id=in_plane(step), device_id_type=MESH,
        )

    def bulk(ref, first, device):
        return pltpu.make_async_remote_copy(
            src_ref=ref, dst_ref=ref,
            send_sem=sems.at[first], recv_sem=sems.at[first + 1],
            device_id=device, device_id_type=MESH,
        )

    up = pltpu.make_async_remote_copy(
        src_ref=x_ref.at[pl.ds(CH - 16, 16)], dst_ref=halo_ref.at[0],
        send_sem=halo_sems.at[0], recv_sem=halo_sems.at[1],
        device_id=on_line(1), device_id_type=MESH,
    )
    down = pltpu.make_async_remote_copy(
        src_ref=x_ref.at[pl.ds(0, 16)], dst_ref=halo_ref.at[1],
        send_sem=halo_sems.at[2], recv_sem=halo_sems.at[3],
        device_id=on_line(-1), device_id_type=MESH,
    )

    for slot, step in enumerate(plane_list):
        to_owner = owner(ys[step[0]], xs[step[1]], nx) == 0
        pl.when(to_owner)(plane_copy(slot, step).start)

    loads[3].wait()
    fir_w[...] = fir_weights(fir_ref)
    win_w[...] = window_weights()
    own_w[...] = own_weights(space_ref, first_channel, count * CH)
    a_ref[SRCS * FINE :, :] = jnp.zeros((256 - SRCS * FINE, a_ref.shape[1]), BF16)

    peer = in_plane(plane_list[0])
    all_plane = bulk(recv1, 0, peer)
    all_z = bulk(recv2, 2, along_z(1))

    def some_sent(n):
        return bulk(send1.at[pl.ds(0, n * own)], 0, peer)

    def some_gathered(n):
        return bulk(gathered.at[pl.ds(0, n * own)], 4, peer)

    all_sent = bulk(recv1, 4, peer)

    @pl.when(is_owner)
    def _():
        all_plane.wait_recv()
        total = send1[pl.ds(mine * own, own)]
        for slot in range(nq - 1):
            total = total + recv1[slot]
        send2[...] = total
        for slot, step in enumerate(z_list):
            z_copy(slot, step).start()

    up.start()
    down.start()

    @pl.when(is_owner)
    def _():
        all_z.wait_recv()
        total = send2[...]
        for slot in range(nz - 1):
            total = total + recv2[slot]
        gathered[pl.ds(mine * own, own)] = total
        for step in plane_list:
            gather_copy(step).start()

    up.wait_recv()
    down.wait_recv()
    high, low = split(jnp.concatenate([x_ref[...], pad, halo_ref[0], halo_ref[1]], axis=0))
    spatial = dot(own_w[...], jnp.concatenate([high, high, low], axis=0))
    blocks = jnp.concatenate(
        [spatial[:, 128 * b : 128 * b + 128] for b in range(BLOCKS)], axis=0
    )
    n_ref[...] = normalized(blocks, CH, fir_w[...], win_w[...])
    lane = iota((CH, 128), 1)
    none = [jnp.zeros((CH, 128), F32)] * COARSE

    def turned_blocks(b):
        if not 0 <= b < BLOCKS:
            return none
        block = n_ref[b * CH : b * CH + CH]
        return [block] + [pltpu.roll(block, 128 - 16 * k, 1) for k in range(1, COARSE)]

    here = none
    for b in range(-1, BLOCKS + 1):
        following = turned_blocks(b + 1)
        shifted = [
            jnp.where(lane < 128 - 16 * k, here[k], following[k]) for k in range(COARSE)
        ]
        q_ref[:, (b + 1) * 128 : (b + 2) * 128] = jnp.concatenate(shifted, axis=0).astype(BF16)
        here = following

    pl.when(is_owner)(lambda: some_gathered(owners - 1).wait_recv())
    pl.when(~is_owner)(lambda: some_gathered(owners).wait_recv())
    pieces = []
    for b in range(BLOCKS):
        rest = gathered[BLOCKS + b // 2]
        pieces += [gathered[b], pltpu.roll(rest, 4, 0) if b % 2 else rest]
    records = jnp.concatenate(pieces, axis=0)
    s_ref[...] = normalized(records, SROWS, fir_w[...], win_w[...])
    shift, lane = iota((FINE, 128), 0), iota((FINE, 128), 1)
    for i in range(SRCS):
        before = jnp.zeros((FINE, 128), F32)
        for b in range(BLOCKS + 1):
            if b < BLOCKS:
                row = b * SROWS + i
                wide = jnp.broadcast_to(s_ref[row : row + 1, :], (FINE, 128))
                here = pltpu.roll(wide, 0, 1, stride=1, stride_axis=0)
            else:
                here = jnp.zeros((FINE, 128), F32)
            a_ref[FINE * i : FINE * i + FINE, 128 * b : 128 * b + 128] = jnp.where(
                lane >= shift, here, before
            ).astype(BF16)
            before = here

    width = (BLOCKS + 1) * 128
    lane = iota((CH, 128), 1)
    factor = float(SAMPLES) ** -0.5
    for half in range(2):
        d = dot(q_ref[:, 128 * half : 128 * half + width], a_ref[...], ((1,), (1,)))
        for tile in range(2):
            v = [
                d[CH * k : CH * k + CH, 128 * tile : 128 * tile + 128] * factor
                for k in range(COARSE)
            ]
            for bit in (1, 2, 4):
                low_part = (lax.div(lane, 16) & bit) == 0
                for k in range(COARSE):
                    if k & bit:
                        continue
                    a, b = v[k], v[k | bit]
                    v[k] = jnp.where(low_part, a, pltpu.roll(b, 16 * bit, 1))
                    v[k | bit] = jnp.where(low_part, pltpu.roll(a, 128 - 16 * bit, 1), b)
            for k in range(COARSE):
                if COARSE * tile + k < SRCS:
                    out_ref[COARSE * tile + k, :, 128 * half : 128 * half + 128] = v[k]

    @pl.when(is_owner)
    def _():
        some_sent(owners - 1).wait_send()
        all_z.wait_send()
        all_sent.wait_send()

    pl.when(~is_owner)(lambda: some_sent(owners).wait_send())
    up.wait_send()
    down.wait_send()


def copy_out(in_ref, out_ref, sem):
    copy = pltpu.make_async_copy(in_ref, out_ref, sem)
    copy.start()
    copy.wait()


def local(nf, ns, nz, strain, fir_taps, space_taps, sources):
    nq = (nf // nz) * ns
    own = PIECES // (nq * 3 // 4)
    width = (BLOCKS + 1) * 128
    hbm = pl.BlockSpec(memory_space=pltpu.HBM)
    result = jax.ShapeDtypeStruct((SRCS, CH, 2 * 128), F32)
    out = pl.pallas_call(
        functools.partial(kernel, nf, ns, nz),
        out_shape=result,
        in_specs=[hbm] * 4,
        out_specs=pl.BlockSpec(memory_space=pltpu.VMEM),
        scratch_shapes=[
            pltpu.SMEM((TAPS,), F32),
            pltpu.SMEM((SPACE,), F32),
            pltpu.SMEM((3, 4), jnp.int32),
            pltpu.VMEM((CH, SAMPLES), F32),
            pltpu.VMEM((2, 16, SAMPLES), F32),
            pltpu.VMEM((PIECES, 8, 128), F32),
            pltpu.VMEM((nq - 1, own, 8, 128), F32),
            pltpu.VMEM((own, 8, 128), F32),
            pltpu.VMEM((nz - 1, own, 8, 128), F32),
            pltpu.VMEM((PIECES, 8, 128), F32),
            pltpu.VMEM((384, 256), BF16),
            pltpu.VMEM((256, 384), BF16),
            pltpu.VMEM((CH, 192), BF16),
            pltpu.VMEM((BLOCKS * CH, 128), F32),
            pltpu.VMEM((BLOCKS * SROWS, 128), F32),
            pltpu.VMEM((COARSE * CH, width + 128), BF16),
            pltpu.VMEM((256, width), BF16),
            pltpu.SemaphoreType.DMA((4,)),
            pltpu.SemaphoreType.DMA((6,)),
            pltpu.SemaphoreType.DMA((4,)),
        ],
        compiler_params=pltpu.CompilerParams(
            collective_id=0, has_side_effects=True, vmem_limit_bytes=16 << 20
        ),
    )(*[pltpu.with_memory_space_constraint(v, pltpu.HBM) for v in (fir_taps, space_taps, sources, strain)])
    out = pl.pallas_call(
        copy_out,
        out_shape=result,
        in_specs=[pl.BlockSpec(memory_space=pltpu.VMEM)],
        out_specs=pl.BlockSpec(memory_space=pltpu.HBM),
        scratch_shapes=[pltpu.SemaphoreType.DMA],
        compiler_params=pltpu.CompilerParams(vmem_limit_bytes=16 << 20),
    )(out)
    return out.reshape(3, 4, CH, 256)


def solution(mesh):
    nf, ns = mesh.shape["fibre"], mesh.shape["seg"]
    nz = 8 if nf % 8 == 0 else 2
    return jax.shard_map(
        functools.partial(local, nf, ns, nz),
        mesh=mesh,
        in_specs=(P(("fibre", "seg"), None), P(), P(), P()),
        out_specs=P(None, None, ("fibre", "seg"), None),
        check_vma=False,
    )
```
